32 devices in a mesh: fsdp: 4 (over z), ctx: 2 (over core), tp: 4 (over y, x).
Axes of the slice: x: 2, y: 2, z: 4, core: 2. Of those that a mesh axis runs over, the one named last changes fastest.
Arguments:
- tokens: bfloat16 [6144, 2048], P(('fsdp', 'ctx')), may hold values from -6 to 6
- cotangent: bfloat16 [6144, 2048], P(('fsdp', 'ctx')), may hold values from -6 to 6
- adapter_ids: int32 [4, 5], replicated, may hold values from 0 to 7
- gain_attn: float32 [2048], replicated, may hold values from 0.5 to 1.5
- gain_mlp: float32 [2048], replicated, may hold values from 0.5 to 1.5
- query_weight: bfloat16 [2048, 2048], P('fsdp', 'tp'), may hold values from -0.125 to 0.125
- key_weight: bfloat16 [2048, 256], P('fsdp', 'tp'), may hold values from -0.125 to 0.125
- value_weight: bfloat16 [2048, 256], P('fsdp', 'tp'), may hold values from -0.125 to 0.125
- output_weight: bfloat16 [2048, 2048], P('tp', 'fsdp'), may hold values from -1 to 1
- gate_weight: bfloat16 [2048, 5632], P('fsdp', 'tp'), may hold values from -0.125 to 0.125
- up_weight: bfloat16 [2048, 5632], P('fsdp', 'tp'), may hold values from -0.125 to 0.125
- down_weight: bfloat16 [5632, 2048], P('tp', 'fsdp'), may hold values from -0.078125 to 0.078125
- query_first: bfloat16 [8, 2048, 16], replicated, may hold values from -0.125 to 0.125
- query_second: bfloat16 [8, 16, 2048], P(None, None, 'tp'), may hold values from -1.5 to 1.5
- key_first: bfloat16 [8, 2048, 16], replicated, may hold values from -0.125 to 0.125
- key_second: bfloat16 [8, 16, 256], P(None, None, 'tp'), may hold values from -1.5 to 1.5
- value_first: bfloat16 [8, 2048, 16], replicated, may hold values from -0.125 to 0.125
- value_second: bfloat16 [8, 16, 256], P(None, None, 'tp'), may hold values from -1.5 to 1.5
- output_first: bfloat16 [8, 2048, 16], P(None, 'tp'), may hold values from -1 to 1
- output_second: bfloat16 [8, 16, 2048], replicated, may hold values from -1.5 to 1.5
- gate_first: bfloat16 [8, 2048, 16], replicated, may hold values from -0.125 to 0.125
- gate_second: bfloat16 [8, 16, 5632], P(None, None, 'tp'), may hold values from -1.5 to 1.5
- up_first: bfloat16 [8, 2048, 16], replicated, may hold values from -0.125 to 0.125
- up_second: bfloat16 [8, 16, 5632], P(None, None, 'tp'), may hold values from -1.5 to 1.5
- down_first: bfloat16 [8, 5632, 16], P(None, 'tp'), may hold values from -0.078125 to 0.078125
- down_second: bfloat16 [8, 16, 2048], replicated, may hold values from -1.5 to 1.5
Outputs:
- output: bfloat16 [6144, 2048], P(('fsdp', 'ctx'))
- input_grad: float32 [6144, 2048], P(('fsdp', 'ctx'))
- query_first_grad: float32 [8, 2048, 16], replicated
- query_second_grad: float32 [8, 16, 2048], P(None, None, 'tp')
- key_first_grad: float32 [8, 2048, 16], replicated
- key_second_grad: float32 [8, 16, 256], P(None, None, 'tp')
- value_first_grad: float32 [8, 2048, 16], replicated
- value_second_grad: float32 [8, 16, 256], P(None, None, 'tp')
- output_first_grad: float32 [8, 2048, 16], P(None, 'tp')
- output_second_grad: float32 [8, 16, 2048], replicated
- gate_first_grad: float32 [8, 2048, 16], replicated
- gate_second_grad: float32 [8, 16, 5632], P(None, None, 'tp')
- up_first_grad: float32 [8, 2048, 16], replicated
- up_second_grad: float32 [8, 16, 5632], P(None, None, 'tp')
- down_first_grad: float32 [8, 5632, 16], P(None, 'tp')
- down_second_grad: float32 [8, 16, 2048], replicated
The draws below stay inside these ranges and needn't reach their ends.
All inputs are finite; a program needn't handle non-finite values.
Results may differ from the reference program's by a relative error of at most 0.019.
The reference program's roundings to bfloat16 on the way count: a program that leaves them out, or rounds other values in their place, can miss the bound.
Values may be sent and summed in bfloat16 or wider, within the bound.
No kernel may reach another device: no remote copies, remote signals or barrier semaphores. Data moves between devices by JAX's collectives and lax.ppermute only.
A program may use at most 112 MiB of HBM per device.

```python
import jax
import jax.numpy as jnp
from jax import lax

D = 2048
HEADS = 32
KV = 4
HD = 64
FF = 5632
RANK = 16
ADAPTERS = 8
PROMPT = 1024
CONT_LEN = 128
SEQS = 5
GROUP = 1536
GROUPS = 4
TOKENS = 6144


def plant(array, own_key, least, top_value):
    longest = array.shape.index(max(array.shape))
    spots = []
    for shift in (0, 1):
        where = [jax.random.randint(jax.random.fold_in(own_key, axis), (), 0, length) for axis, length in enumerate(array.shape)]
        where[longest] = (where[longest] + shift) % array.shape[longest]
        spots.append(tuple(where))
    return array.at[spots[0]].set(least).at[spots[1]].set(top_value)


def block_levels(own_key, dims, shards, smallest, largest):
    level, own = 1.0, jax.random.fold_in(own_key, 6)
    for dim, shards_of in shards:
        steps = jnp.exp(jax.random.uniform(jax.random.fold_in(own, dim), (shards_of,), jnp.float32, smallest / len(shards), largest / len(shards)))
        level = level * jnp.repeat(steps, dims[dim] // shards_of).reshape([-1 if axis == dim else 1 for axis in range(len(dims))])
    return level


def normal_values(stream_key, extent, width, most, cuts=(), kind=jnp.bfloat16):
    array = jax.random.normal(stream_key, extent, jnp.float32) * width
    if len(cuts) > 0:
        array = block_levels(stream_key, extent, cuts, -0.22, 0.18) * array
    return jnp.clip(array, min=-most, max=most).astype(kind)


def setup_inputs(seed: int = 0) -> dict:
    key_of = jax.random.split(jax.random.key(seed), 27)
    return {
        "tokens": normal_values(key_of[0], (TOKENS, D), 1.0, 6.0, ((0, 8),)),
        "cotangent": normal_values(key_of[1], (TOKENS, D), 1.0, 6.0, ((0, 8),)),
        "adapter_ids": plant(jax.random.randint(key_of[2], (GROUPS, SEQS), 0, ADAPTERS), jax.random.fold_in(key_of[2], 1), 0, ADAPTERS - 1).astype(jnp.int32),
        "gain_attn": jnp.clip(1.0 + 0.1 * jax.random.normal(key_of[3], (D,), jnp.float32), 0.5, 1.5),
        "gain_mlp": jnp.clip(1.0 + 0.1 * jax.random.normal(key_of[4], (D,), jnp.float32), 0.5, 1.5),
        "query_weight": normal_values(key_of[5], (D, HEADS * HD), D ** -0.5, 0.125, ((0, 4), (1, 4))),
        "key_weight": normal_values(key_of[6], (D, KV * HD), D ** -0.5, 0.125, ((0, 4), (1, 4))),
        "value_weight": normal_values(key_of[7], (D, KV * HD), D ** -0.5, 0.125, ((0, 4), (1, 4))),
        "output_weight": normal_values(key_of[8], (HEADS * HD, D), (HEADS * HD // 64) ** -0.5, 1.0, ((0, 4), (1, 4))),
        "gate_weight": normal_values(key_of[9], (D, FF), D ** -0.5, 0.125, ((0, 4), (1, 4))),
        "up_weight": normal_values(key_of[10], (D, FF), D ** -0.5, 0.125, ((0, 4), (1, 4))),
        "down_weight": normal_values(key_of[11], (FF, D), FF ** -0.5, 0.078125, ((0, 4), (1, 4))),
        "query_first": normal_values(key_of[12], (ADAPTERS, D, RANK), D ** -0.5, 0.125),
        "query_second": normal_values(key_of[13], (ADAPTERS, RANK, HEADS * HD), RANK ** -0.5, 1.5, ((2, 4),)),
        "key_first": normal_values(key_of[14], (ADAPTERS, D, RANK), D ** -0.5, 0.125),
        "key_second": normal_values(key_of[15], (ADAPTERS, RANK, KV * HD), RANK ** -0.5, 1.5, ((2, 4),)),
        "value_first": normal_values(key_of[16], (ADAPTERS, D, RANK), D ** -0.5, 0.125),
        "value_second": normal_values(key_of[17], (ADAPTERS, RANK, KV * HD), RANK ** -0.5, 1.5, ((2, 4),)),
        "output_first": normal_values(key_of[18], (ADAPTERS, HEADS * HD, RANK), (HEADS * HD // 64) ** -0.5, 1.0, ((1, 4),)),
        "output_second": normal_values(key_of[19], (ADAPTERS, RANK, D), RANK ** -0.5, 1.5),
        "gate_first": normal_values(key_of[20], (ADAPTERS, D, RANK), D ** -0.5, 0.125),
        "gate_second": normal_values(key_of[21], (ADAPTERS, RANK, FF), RANK ** -0.5, 1.5, ((2, 4),)),
        "up_first": normal_values(key_of[22], (ADAPTERS, D, RANK), D ** -0.5, 0.125),
        "up_second": normal_values(key_of[23], (ADAPTERS, RANK, FF), RANK ** -0.5, 1.5, ((2, 4),)),
        "down_first": normal_values(key_of[24], (ADAPTERS, FF, RANK), FF ** -0.5, 0.078125, ((1, 4),)),
        "down_second": normal_values(key_of[25], (ADAPTERS, RANK, D), RANK ** -0.5, 1.5),
    }


EPS = 1e-05
SCALE = 0.125
THETA = 10000.0

@jax.custom_vjp
def low(v):
    return lax.optimization_barrier(v.astype(jnp.bfloat16)).astype(jnp.float32)

@jax.custom_vjp
def low_back(v):
    return v

def low_keep(v):
    return (low(v), None)

def low_pass(kept, grad):
    return (grad,)

def back_keep(v):
    return (v, None)

def back_low(kept, grad):
    return (low(grad),)
low.defvjp(low_keep, low_pass)
low_back.defvjp(back_keep, back_low)

def matmul(left, right):
    return jnp.dot(left, right, precision=lax.Precision.HIGHEST)

def layout(stream):
    in_prompt = stream < PROMPT
    later = jnp.maximum(stream - PROMPT, 0)
    sequence = jnp.where(in_prompt, 0, 1 + later // CONT_LEN).astype(jnp.int32)
    position = jnp.where(in_prompt, stream, PROMPT + later % CONT_LEN).astype(jnp.int32)
    return (sequence, position)

def selector(sequence, row_ids):
    places = jnp.arange(row_ids.shape[0], dtype=jnp.int32)
    chosen = lax.optimization_barrier(jnp.sum(jnp.where(sequence[:, None] == places[None, :], row_ids[None, :], 0), axis=1))
    columns = jnp.arange(ADAPTERS * RANK, dtype=jnp.int32) // RANK
    return (chosen[:, None] == columns[None, :]).astype(jnp.float32)

def angles(position):
    freqs = THETA ** (-(jnp.arange(HD // 2, dtype=jnp.int32) * 2).astype(jnp.float32) / HD)
    turned = position.astype(jnp.float32)[:, None] * freqs[None, :]
    return (jnp.cos(turned), jnp.sin(turned))

def rotate(values, cosine, sine):
    half = values.shape[-1] // 2
    first = values[..., :half]
    second = values[..., half:]
    return jnp.concatenate([first * cosine - second * sine, second * cosine + first * sine], axis=-1)

def flat_first(first):
    return jnp.transpose(first, (1, 0, 2)).reshape(first.shape[1], first.shape[0] * first.shape[2])

def flat_second(second):
    return second.reshape(second.shape[0] * second.shape[1], second.shape[2])

def adapted(source, weight, first, second, select):
    inner = low(low_back(matmul(source, flat_first(first)) * select))
    return matmul(source, weight) + matmul(inner, flat_second(second))

def rms(values, gain):
    return values * lax.rsqrt(lax.optimization_barrier(jnp.mean(values * values, axis=1, keepdims=True)) + EPS) * gain

def group_forward(frozen, adapters, source, row_ids):
    gain_attn, gain_mlp, query_weight, key_weight, value_weight, output_weight, gate_weight, up_weight, down_weight = frozen
    query_first, query_second, key_first, key_second, value_first, value_second, output_first, output_second, gate_first, gate_second, up_first, up_second, down_first, down_second = adapters
    stream = jnp.arange(GROUP, dtype=jnp.int32)
    sequence, position = layout(stream)
    select = selector(sequence, row_ids)
    cosine, sine = angles(position)
    normed = low(rms(source, gain_attn))
    query = adapted(normed, query_weight, query_first, query_second, select)
    key = adapted(normed, key_weight, key_first, key_second, select)
    value = adapted(normed, value_weight, value_first, value_second, select)
    query = low(rotate(low_back(query).reshape(GROUP, HEADS, HD), cosine[:, None, :], sine[:, None, :]))
    key = low(rotate(low_back(key).reshape(GROUP, KV, HD), cosine[:, None, :], sine[:, None, :]))
    value = low(low_back(value)).reshape(GROUP, KV, HD)
    allowed = (stream[None, :] <= stream[:, None]) & ((stream[None, :] < PROMPT) | (sequence[None, :] == sequence[:, None]))
    query_heads = jnp.transpose(query, (1, 0, 2))
    key_heads = jnp.transpose(jnp.repeat(key, HEADS // KV, axis=1), (1, 0, 2))
    value_heads = jnp.transpose(jnp.repeat(value, HEADS // KV, axis=1), (1, 0, 2))

    def one_head(operands):
        query_one, key_one, value_one = operands
        scores = low_back(matmul(query_one, key_one.T) * SCALE)
        scores = jnp.where(allowed, scores, -1e+30)
        probs = jax.nn.softmax(scores, axis=1)
        return matmul(low(probs), value_one)
    attended = lax.map(jax.checkpoint(one_head), (query_heads, key_heads, value_heads))
    attended = low(low_back(jnp.transpose(attended, (1, 0, 2)).reshape(GROUP, HEADS * HD)))
    out_inner = low(low_back(matmul(attended, flat_first(output_first)) * select))
    branch = low_back(matmul(attended, output_weight) + matmul(out_inner, flat_second(output_second)))
    middle = source + branch
    normed_two = low(rms(middle, gain_mlp))
    gate = low_back(adapted(normed_two, gate_weight, gate_first, gate_second, select))
    upper = low_back(adapted(normed_two, up_weight, up_first, up_second, select))
    hidden = low(jax.nn.silu(gate) * upper)
    down_inner = low(low_back(matmul(hidden, flat_first(down_first)) * select))
    feed = low_back(matmul(hidden, down_weight) + matmul(down_inner, flat_second(down_second)))
    return middle + feed

def reference(tokens, cotangent, adapter_ids, gain_attn, gain_mlp, query_weight, key_weight, value_weight, output_weight, gate_weight, up_weight, down_weight, query_first, query_second, key_first, key_second, value_first, value_second, output_first, output_second, gate_first, gate_second, up_first, up_second, down_first, down_second):
    frozen = tuple((a.astype(jnp.float32) for a in (gain_attn, gain_mlp, query_weight, key_weight, value_weight, output_weight, gate_weight, up_weight, down_weight)))
    adapters = tuple((a.astype(jnp.float32) for a in (query_first, query_second, key_first, key_second, value_first, value_second, output_first, output_second, gate_first, gate_second, up_first, up_second, down_first, down_second)))
    source = tokens.astype(jnp.float32).reshape(GROUPS, GROUP, D)
    upstream = cotangent.astype(jnp.float32).reshape(GROUPS, GROUP, D)

    def forward(source_all, adapter_all):
        return lax.map(lambda item: group_forward(frozen, adapter_all, item[0], item[1]), (source_all, adapter_ids))
    result, pullback = jax.vjp(forward, source, adapters)
    grad_source, grad_adapters = pullback(upstream)
    output = result.reshape(TOKENS, D).astype(jnp.bfloat16)
    input_grad = grad_source.reshape(TOKENS, D).astype(jnp.float32)
    g = grad_adapters
    return (output, input_grad, g[0], g[1], g[2], g[3], g[4], g[5], g[6], g[7], g[8], g[9], g[10], g[11], g[12], g[13])
```

```python
import functools

import jax
import jax.numpy as jnp
from jax import lax
from jax.experimental import pallas as pl
from jax.experimental.pallas import tpu as pltpu
from jax.sharding import PartitionSpec as P

HD = 64
RANK = 16
ADAPTERS = 8
PROMPT = 1024
CONT_LEN = 128
GROUP = 1536
BLOCK = 256


EPS = 1e-05
SCALE = 0.125
THETA = 10000.0
F32 = jnp.float32
BF16 = jnp.bfloat16


def dot(left, right, left_dim, right_dim):
    return lax.dot_general(
        left, right, (((left_dim,), (right_dim,)), ((), ())), preferred_element_type=F32
    )


def nn(left, right):
    return dot(left, right, 1, 0)


def nt(left, right):
    return dot(left, right, 1, 1)


def tn(left, right):
    return dot(left, right, 0, 0)


def layout(stream):
    in_prompt = stream < PROMPT
    later = jnp.maximum(stream - PROMPT, 0)
    sequence = jnp.where(in_prompt, 0, 1 + later // CONT_LEN)
    position = jnp.where(in_prompt, stream, PROMPT + later % CONT_LEN)
    return (sequence, position)


def selector(sequence, row_ids):
    places = jnp.arange(row_ids.shape[0], dtype=jnp.int32)
    chosen = jnp.sum(jnp.where(sequence[:, None] == places[None, :], row_ids[None, :], 0), axis=1)
    columns = jnp.arange(ADAPTERS * RANK, dtype=jnp.int32) // RANK
    return (chosen[:, None] == columns[None, :]).astype(F32)


def angles(position):
    freqs = THETA ** (-(jnp.arange(HD // 2, dtype=jnp.int32) * 2).astype(F32) / HD)
    turned = freqs[:, None] * position.astype(F32)[None, :]
    return (jnp.cos(turned), jnp.sin(turned))


def rotate(values, cosine, sine):
    half = HD // 2
    heads = values.shape[0] // HD
    split = values.reshape(heads, 2, half, values.shape[1])
    first = split[:, 0]
    second = split[:, 1]
    turned = jnp.stack(
        [first * cosine - second * sine, second * cosine + first * sine], axis=1
    )
    return turned.reshape(values.shape)


def first_rows(first):
    return jnp.transpose(first, (0, 2, 1)).reshape(first.shape[0] * first.shape[2], first.shape[1])


def second_rows(second):
    return second.reshape(second.shape[0] * second.shape[1], second.shape[2])


def unfirst(grad):
    return jnp.transpose(grad.reshape(ADAPTERS, RANK, grad.shape[1]), (0, 2, 1))


def unsecond(grad):
    return grad.reshape(ADAPTERS, RANK, grad.shape[1])


def rms_back(values, scaling, gain, grad_normed):
    weighted = grad_normed * gain
    return scaling * weighted - values * scaling * scaling * scaling * jnp.mean(
        weighted * values, axis=1, keepdims=True
    )


def diagonal_mask(block):
    key_at = lax.broadcasted_iota(jnp.int32, (BLOCK, BLOCK), 0)
    query_at = lax.broadcasted_iota(jnp.int32, (BLOCK, BLOCK), 1)
    same = (key_at // CONT_LEN) == (query_at // CONT_LEN)
    return (key_at <= query_at) & ((block < PROMPT // BLOCK) | same)


def forward_kernel(first_ref, k_ref, vt_ref, qt_ref, o_ref, lse_ref):
    block = first_ref[0] + pl.program_id(0)
    query = qt_ref[0]
    at = pl.multiple_of(block * BLOCK, BLOCK)
    masked = jnp.where(
        diagonal_mask(block), nn(k_ref[pl.ds(at, BLOCK), :], query) * SCALE, -1e30
    )
    value_own = vt_ref[:, pl.ds(at, BLOCK)]

    def finish(count):
        largest = jnp.max(masked, axis=0, keepdims=True)
        if count:
            scores = nn(k_ref[: count * BLOCK, :], query) * SCALE
            largest = jnp.maximum(largest, jnp.max(scores, axis=0, keepdims=True))
        expo = jnp.exp(masked - largest)
        total = jnp.sum(expo, axis=0, keepdims=True)
        out = nn(value_own, expo.astype(BF16))
        if count:
            expo = jnp.exp(scores - largest)
            total = total + jnp.sum(expo, axis=0, keepdims=True)
            out = out + nn(vt_ref[:, : count * BLOCK], expo.astype(BF16))
        o_ref[0] = (out / total).astype(BF16)
        lse_ref[0] = largest + jnp.log(total)

    seen = jnp.minimum(block, PROMPT // BLOCK)
    for count in range(PROMPT // BLOCK + 1):
        pl.when(seen == count)(functools.partial(finish, count))


def attend(first, key, value_t, query_t):
    heads, _, rows = query_t.shape
    whole = key.shape[0]
    spec = pl.BlockSpec((1, HD, BLOCK), lambda i, h, f: (h, 0, i))
    return pl.pallas_call(
        forward_kernel,
        out_shape=(
            jax.ShapeDtypeStruct((heads, HD, rows), BF16),
            jax.ShapeDtypeStruct((heads, 1, rows), F32),
        ),
        grid_spec=pltpu.PrefetchScalarGridSpec(
            num_scalar_prefetch=1,
            grid=(rows // BLOCK, heads),
            in_specs=[
                pl.BlockSpec((whole, HD), lambda i, h, f: (0, 0)),
                pl.BlockSpec((HD, whole), lambda i, h, f: (0, 0)),
                spec,
            ],
            out_specs=(spec, pl.BlockSpec((1, 1, BLOCK), lambda i, h, f: (h, 0, i))),
        ),
        cost_estimate=pl.CostEstimate(
            flops=heads * rows * whole * HD * 4,
            bytes_accessed=heads * rows * HD * 4,
            transcendentals=heads * rows * whole,
        ),
    )(first, key, value_t, query_t)


def backward_kernel(
    first_ref, k_ref, v_ref, kt_ref, qt_ref, ot_ref, dot_ref, lse_ref, dq_ref, dkv_ref
):
    block = first_ref[0] + pl.program_id(0)

    @pl.when((pl.program_id(0) == 0) & (pl.program_id(1) == 0))
    def _():
        dkv_ref[...] = jnp.zeros_like(dkv_ref)

    query = qt_ref[0]
    grad = dot_ref[0]
    logs = lse_ref[0]
    delta = jnp.sum(grad.astype(F32) * ot_ref[0].astype(F32), axis=0, keepdims=True)
    at = pl.multiple_of(block * BLOCK, BLOCK)

    def part(key_rows, value_rows, allowed):
        scores = nn(key_rows, query) * SCALE
        if allowed is not None:
            scores = jnp.where(allowed, scores, -1e30)
        probs = jnp.exp(scores - logs)
        grad_probs = nn(value_rows, grad)
        grad_scores = (probs * (grad_probs - delta)).astype(BF16)
        return (
            grad_scores,
            nt(query, grad_scores) * SCALE,
            nt(grad, probs.astype(BF16)),
        )

    def finish(count):
        own = pl.ds(at, BLOCK)
        grad_scores, grad_key, grad_value = part(
            k_ref[own, :], v_ref[own, :], diagonal_mask(block)
        )
        dkv_ref[:HD, own] += grad_key
        dkv_ref[HD:, own] += grad_value
        grad_query = nn(kt_ref[:, own], grad_scores)
        if count:
            grad_scores, grad_key, grad_value = part(
                k_ref[: count * BLOCK, :], v_ref[: count * BLOCK, :], None
            )
            dkv_ref[:HD, : count * BLOCK] += grad_key
            dkv_ref[HD:, : count * BLOCK] += grad_value
            grad_query = grad_query + nn(kt_ref[:, : count * BLOCK], grad_scores)
        dq_ref[0] = grad_query * SCALE

    seen = jnp.minimum(block, PROMPT // BLOCK)
    for count in range(PROMPT // BLOCK + 1):
        pl.when(seen == count)(functools.partial(finish, count))


def attend_back(first, key, value, key_t, query_t, out_t, grad_t, logs):
    heads, _, rows = query_t.shape
    whole = key.shape[0]
    spec = pl.BlockSpec((1, HD, BLOCK), lambda i, h, f: (h, 0, i))
    row = pl.BlockSpec((whole, HD), lambda i, h, f: (0, 0))
    return pl.pallas_call(
        backward_kernel,
        out_shape=(
            jax.ShapeDtypeStruct((heads, HD, rows), F32),
            jax.ShapeDtypeStruct((2 * HD, whole), F32),
        ),
        grid_spec=pltpu.PrefetchScalarGridSpec(
            num_scalar_prefetch=1,
            grid=(rows // BLOCK, heads),
            in_specs=[
                row,
                row,
                pl.BlockSpec((HD, whole), lambda i, h, f: (0, 0)),
                spec,
                spec,
                spec,
                pl.BlockSpec((1, 1, BLOCK), lambda i, h, f: (h, 0, i)),
            ],
            out_specs=(spec, pl.BlockSpec((2 * HD, whole), lambda i, h, f: (0, 0))),
        ),
        cost_estimate=pl.CostEstimate(
            flops=heads * rows * whole * HD * 10,
            bytes_accessed=heads * rows * HD * 10,
            transcendentals=heads * rows * whole,
        ),
    )(first, key, value, key_t, query_t, out_t, grad_t, logs)


def flipped(bit):
    return [(place, place ^ bit) for place in range(4)]


def bit_of(bit):
    return (lax.axis_index("tp") // bit) % 2


def reduce_rows(partial, bit):
    other = 3 - bit
    half = partial.shape[0] // 2
    quarter = half // 2
    mine = bit_of(bit)
    then = bit_of(other)
    sent = lax.dynamic_slice_in_dim(partial, (1 - mine) * half, half, 0)
    kept = lax.dynamic_slice_in_dim(partial, mine * half, half, 0)
    came = lax.ppermute(sent, "tp", flipped(bit))
    summed = kept.astype(F32) + came.astype(F32)
    sent = lax.dynamic_slice_in_dim(summed, (1 - then) * quarter, quarter, 0).astype(BF16)
    kept = lax.dynamic_slice_in_dim(summed, then * quarter, quarter, 0)
    came = lax.ppermute(sent, "tp", flipped(other))
    return kept + came.astype(F32)


def gather_rows(own, bit):
    other = 3 - bit
    mine = bit_of(bit)
    then = bit_of(other)
    came = lax.ppermute(own, "tp", flipped(other))
    pair = jnp.where(
        then == 0, jnp.concatenate([own, came], axis=0), jnp.concatenate([came, own], axis=0)
    )
    came = lax.ppermute(pair, "tp", flipped(bit))
    return jnp.where(
        mine == 0, jnp.concatenate([pair, came], axis=0), jnp.concatenate([came, pair], axis=0)
    )


def shards(
    tokens,
    cotangent,
    adapter_ids,
    gain_attn,
    gain_mlp,
    query_weight,
    key_weight,
    value_weight,
    output_weight,
    gate_weight,
    up_weight,
    down_weight,
    query_first,
    query_second,
    key_first,
    key_second,
    value_first,
    value_second,
    output_first,
    output_second,
    gate_first,
    gate_second,
    up_first,
    up_second,
    down_first,
    down_second,
):
    rows, width = tokens.shape
    q_width = query_weight.shape[1]
    heads = q_width // HD
    inner = ADAPTERS * RANK
    core = lax.axis_index("ctx")
    place = lax.axis_index("tp")
    stream = core * rows + jnp.arange(rows, dtype=jnp.int32)
    sequence, position = layout(stream)
    row_ids = lax.dynamic_index_in_dim(adapter_ids, lax.axis_index("fsdp"), 0, False)
    select = selector(sequence, row_ids)
    select_low = select.astype(BF16)
    cosine, sine = angles(position)
    first_block = (core * (rows // BLOCK)).astype(jnp.int32).reshape(1)
    chunk = rows // 2
    bits = (1, 2)
    starts = [
        index * chunk + bit_of(bit) * (chunk // 2) + bit_of(3 - bit) * (chunk // 4)
        for index, bit in enumerate(bits)
    ]

    def own_rows(array, index):
        return lax.dynamic_slice_in_dim(array, starts[index], chunk // 4, 0)

    def chunk_of(array, index):
        return lax.slice_in_dim(array, index * chunk, (index + 1) * chunk, axis=0)

    def gathered(local):
        half = local.shape[0] // 2
        part = lax.dynamic_slice_in_dim(local, core * half, half, 0)
        return lax.all_gather(part, ("fsdp", "ctx"), axis=0, tiled=True)

    qkv_full = gathered(jnp.concatenate([query_weight, key_weight, value_weight], axis=1))
    output_full = gathered(output_weight.T)
    gate_full = gathered(gate_weight)
    up_full = gathered(up_weight)
    down_full = gathered(down_weight.T)

    firsts = jnp.concatenate(
        [first_rows(query_first), first_rows(key_first), first_rows(value_first)], axis=0
    )
    query_rows = second_rows(query_second)
    key_rows = second_rows(key_second)
    value_rows = second_rows(value_second)
    output_rows = second_rows(output_second)
    gate_rows = second_rows(gate_second)
    up_rows = second_rows(up_second)
    down_rows = second_rows(down_second)
    output_cols = first_rows(output_first)
    gate_cols = first_rows(gate_first)
    up_cols = first_rows(up_first)
    down_cols = first_rows(down_first)

    source = tokens.astype(F32)
    scale_one = lax.rsqrt(jnp.mean(source * source, axis=1, keepdims=True) + EPS)
    normed = (source * scale_one * gain_attn).astype(BF16)
    triple = jnp.concatenate([select, select, select], axis=1)
    qkv_inner = (nt(normed, firsts) * triple).astype(BF16)
    query_inner = qkv_inner[:, :inner]
    key_inner = qkv_inner[:, inner : 2 * inner]
    value_inner = qkv_inner[:, 2 * inner :]
    projected = dot(qkv_full, normed, 0, 1)
    query_t = projected[:q_width] + dot(query_rows, query_inner, 0, 1)
    key_t = projected[q_width : q_width + HD] + dot(key_rows, key_inner, 0, 1)
    value_t = projected[q_width + HD :] + dot(value_rows, value_inner, 0, 1)
    query_rot = rotate(query_t, cosine, sine).astype(BF16).reshape(heads, HD, rows)
    kv_local = jnp.concatenate([rotate(key_t, cosine, sine), value_t], axis=0).astype(BF16)
    kv_other = lax.ppermute(kv_local, "ctx", [(0, 1), (1, 0)])
    kv_t = jnp.where(
        core == 0,
        jnp.concatenate([kv_local, kv_other], axis=1),
        jnp.concatenate([kv_other, kv_local], axis=1),
    )
    key_whole = kv_t[:HD].T
    value_whole = kv_t[HD:].T
    attended_t, log_total = attend(first_block, key_whole, kv_t[HD:], query_rot)
    att_t = attended_t.reshape(q_width, rows)

    middle, scale_two, spread = [], [], []
    out_weights = jnp.concatenate([output_full, output_cols], axis=0)
    for index, bit in enumerate(bits):
        cols = lax.slice_in_dim(att_t, index * chunk, (index + 1) * chunk, axis=1)
        total = reduce_rows(dot(cols, out_weights, 0, 1).astype(BF16), bit)
        out_inner = (total[:, width:] * own_rows(select, index)).astype(BF16)
        mid = own_rows(tokens, index).astype(F32) + total[:, :width] + nn(out_inner, output_rows)
        scaling = lax.rsqrt(jnp.mean(mid * mid, axis=1, keepdims=True) + EPS)
        normed_own = (mid * scaling * gain_mlp).astype(BF16)
        middle.append(mid)
        scale_two.append(scaling)
        spread.append(gather_rows(jnp.concatenate([normed_own, out_inner], axis=1), bit))

    grad_down_inner = nt(cotangent, down_rows).astype(BF16) * select_low
    hidden_all, grad_gate_all, grad_upper_all, gate_inner_all, up_inner_all = [], [], [], [], []
    back_parts, down_parts = [], []
    inner_cols = jnp.concatenate([gate_cols, up_cols], axis=0)
    for index, bit in enumerate(bits):
        normed_two = spread[index][:, :width]
        sel = chunk_of(select, index)
        both = nt(normed_two, inner_cols)
        gate_inner = (both[:, :inner] * sel).astype(BF16)
        up_inner = (both[:, inner:] * sel).astype(BF16)
        gate = nn(normed_two, gate_full) + nn(gate_inner, gate_rows)
        upper = nn(normed_two, up_full) + nn(up_inner, up_rows)
        sigmoid = jax.nn.sigmoid(gate)
        swish = gate * sigmoid
        hidden = (swish * upper).astype(BF16)
        grad_hidden = nn(chunk_of(cotangent, index), down_full) + nn(
            chunk_of(grad_down_inner, index), down_cols
        )
        grad_gate = (grad_hidden * upper * (sigmoid * (1.0 + gate * (1.0 - sigmoid)))).astype(BF16)
        grad_upper = (grad_hidden * swish).astype(BF16)
        back_parts.append(
            jnp.concatenate(
                [
                    (nt(grad_gate, gate_full) + nt(grad_upper, up_full)).astype(BF16),
                    nt(grad_gate, gate_rows).astype(BF16),
                    nt(grad_upper, up_rows).astype(BF16),
                ],
                axis=1,
            )
        )
        down_parts.append(
            jnp.concatenate(
                [nt(hidden, down_full).astype(BF16), nt(hidden, down_cols).astype(BF16)], axis=1
            )
        )
        hidden_all.append(hidden)
        grad_gate_all.append(grad_gate)
        grad_upper_all.append(grad_upper)
        gate_inner_all.append(gate_inner)
        up_inner_all.append(up_inner)

    grad_middle, grad_spread = [], []
    for index, bit in enumerate(bits):
        total = reduce_rows(back_parts[index], bit)
        sel = own_rows(select_low, index)
        grad_gate_inner = total[:, width : width + inner].astype(BF16) * sel
        grad_up_inner = total[:, width + inner :].astype(BF16) * sel
        grad_normed = total[:, :width] + nn(grad_gate_inner, gate_cols) + nn(grad_up_inner, up_cols)
        grad_mid = own_rows(cotangent, index).astype(F32) + rms_back(
            middle[index], scale_two[index], gain_mlp, grad_normed
        )
        grad_middle.append(grad_mid)
        grad_spread.append(
            gather_rows(
                jnp.concatenate([grad_mid.astype(BF16), grad_gate_inner, grad_up_inner], axis=1),
                bit,
            )
        )

    grad_att_t, grad_out_inner = [], []
    for index in range(2):
        branch = grad_spread[index][:, :width]
        grad_inner = nt(branch, output_rows).astype(BF16) * chunk_of(select_low, index)
        grad_out_inner.append(grad_inner)
        grad_att_t.append(
            (dot(output_full, branch, 0, 1) + dot(output_cols, grad_inner, 0, 1)).astype(BF16)
        )
    grad_heads = jnp.concatenate(grad_att_t, axis=1).reshape(heads, HD, rows)
    grad_query_rot, kv_grad = attend_back(
        first_block,
        key_whole,
        value_whole,
        kv_t[:HD],
        query_rot,
        attended_t,
        grad_heads,
        log_total,
    )
    sent = lax.dynamic_slice_in_dim(kv_grad, (1 - core) * rows, rows, 1)
    kept = lax.dynamic_slice_in_dim(kv_grad, core * rows, rows, 1)
    kv_sum = kept + lax.ppermute(sent, "ctx", [(0, 1), (1, 0)])
    grad_query_t = rotate(grad_query_rot.reshape(q_width, rows), cosine, -sine).astype(BF16)
    grad_key_t = rotate(kv_sum[:HD], cosine, -sine).astype(BF16)
    grad_value_t = kv_sum[HD:].astype(BF16)
    grad_qkv_t = jnp.concatenate([grad_query_t, grad_key_t, grad_value_t], axis=0)

    input_parts, qkv_spread = [], []
    for index, bit in enumerate(bits):
        cols = lax.slice_in_dim(grad_qkv_t, index * chunk, (index + 1) * chunk, axis=1)
        part = jnp.concatenate(
            [
                dot(cols, qkv_full, 0, 1).astype(BF16),
                dot(cols[:q_width], query_rows, 0, 1).astype(BF16),
                dot(cols[q_width : q_width + HD], key_rows, 0, 1).astype(BF16),
                dot(cols[q_width + HD :], value_rows, 0, 1).astype(BF16),
            ],
            axis=1,
        )
        total = reduce_rows(part, bit)
        sel = own_rows(select_low, index)
        inners = total[:, width:].astype(BF16) * jnp.concatenate([sel, sel, sel], axis=1)
        grad_normed = total[:, :width] + nn(inners, firsts)
        own = grad_middle[index] + rms_back(
            own_rows(tokens, index).astype(F32),
            own_rows(scale_one, index),
            gain_attn,
            grad_normed,
        )
        whole = gather_rows(jnp.concatenate([own.astype(BF16), inners], axis=1), bit)
        input_parts.append(whole[:, :width].astype(F32))
        qkv_spread.append(whole[:, width:])
    input_grad = jnp.concatenate(input_parts, axis=0)

    output_parts, down_inner_all = [], []
    for index, bit in enumerate(bits):
        total = reduce_rows(down_parts[index], bit)
        down_inner = (total[:, width:] * own_rows(select, index)).astype(BF16)
        own = middle[index] + total[:, :width] + nn(down_inner, down_rows)
        whole = gather_rows(jnp.concatenate([own.astype(BF16), down_inner], axis=1), bit)
        output_parts.append(whole[:, :width])
        down_inner_all.append(whole[:, width:])
    output = jnp.concatenate(output_parts, axis=0)

    quarter = inner // 4

    def share(array):
        return lax.dynamic_slice_in_dim(array, place * quarter, quarter, 1)

    join = functools.partial(jnp.concatenate, axis=0)
    spread_two = join(spread)
    normed_two = spread_two[:, :width]
    out_inner = spread_two[:, width:]
    back_two = join(grad_spread)
    branch = back_two[:, :width]
    inner_two = back_two[:, width:]
    down_inner = join(down_inner_all)
    hidden = join(hidden_all)
    grad_gate = join(grad_gate_all)
    grad_upper = join(grad_upper_all)
    early = (
        tn(share(inner_two[:, :inner]), normed_two),
        tn(share(inner_two[:, inner:]), normed_two),
        tn(share(out_inner), branch),
        tn(share(down_inner), cotangent),
        tn(grad_down_inner, hidden),
        tn(join(gate_inner_all), grad_gate),
        tn(join(up_inner_all), grad_upper),
        dot(join(grad_out_inner), att_t, 0, 1),
    )
    early = lax.psum(tuple(a.astype(BF16) for a in early), ("fsdp", "ctx"))
    shared = lax.all_gather(jnp.concatenate(early[:4], axis=1), "tp", axis=0, tiled=True)
    gate_first_grad, up_first_grad, output_second_grad, down_second_grad = (
        lax.slice_in_dim(shared, i * width, (i + 1) * width, axis=1).astype(F32) for i in range(4)
    )
    down_first_grad, gate_second_grad, up_second_grad, output_first_grad = (
        a.astype(F32) for a in early[4:]
    )
    inners = join(qkv_spread)
    late = (
        tn(share(inners[:, :inner]), normed),
        tn(share(inners[:, inner : 2 * inner]), normed),
        tn(share(inners[:, 2 * inner :]), normed),
        dot(query_inner, grad_query_t, 0, 1),
        dot(jnp.concatenate([key_inner, value_inner], axis=1), grad_qkv_t[q_width:], 0, 1),
    )
    late = lax.psum(tuple(a.astype(BF16) for a in late), ("fsdp", "ctx"))
    shared = lax.all_gather(jnp.concatenate(late[:3], axis=1), "tp", axis=0, tiled=True)
    query_first_grad, key_first_grad, value_first_grad = (
        lax.slice_in_dim(shared, i * width, (i + 1) * width, axis=1).astype(F32) for i in range(3)
    )
    query_second_grad = late[3].astype(F32)
    key_second_grad = late[4][:inner, :HD].astype(F32)
    value_second_grad = late[4][inner:, HD:].astype(F32)
    return (
        output,
        input_grad,
        unfirst(query_first_grad),
        unsecond(query_second_grad),
        unfirst(key_first_grad),
        unsecond(key_second_grad),
        unfirst(value_first_grad),
        unsecond(value_second_grad),
        unfirst(output_first_grad),
        unsecond(output_second_grad),
        unfirst(gate_first_grad),
        unsecond(gate_second_grad),
        unfirst(up_first_grad),
        unsecond(up_second_grad),
        unfirst(down_first_grad),
        unsecond(down_second_grad),
    )


def solution(mesh):
    placed = (
        P(("fsdp", "ctx"), None),
        P(("fsdp", "ctx"), None),
        P(),
        P(),
        P(),
        P("fsdp", "tp"),
        P("fsdp", "tp"),
        P("fsdp", "tp"),
        P("tp", "fsdp"),
        P("fsdp", "tp"),
        P("fsdp", "tp"),
        P("tp", "fsdp"),
        P(),
        P(None, None, "tp"),
        P(),
        P(None, None, "tp"),
        P(),
        P(None, None, "tp"),
        P(None, "tp", None),
        P(),
        P(),
        P(None, None, "tp"),
        P(),
        P(None, None, "tp"),
        P(None, "tp", None),
        P(),
    )
    return jax.shard_map(
        shards,
        mesh=mesh,
        in_specs=placed,
        out_specs=(
            P(("fsdp", "ctx"), None),
            P(("fsdp", "ctx"), None),
            P(),
            P(None, None, "tp"),
            P(),
            P(None, None, "tp"),
            P(),
            P(None, None, "tp"),
            P(None, "tp", None),
            P(),
            P(),
            P(None, None, "tp"),
            P(),
            P(None, None, "tp"),
            P(None, "tp", None),
            P(),
        ),
        check_vma=False,
    )
```
